32 devices in a mesh: blk: 8 (over y, x, core), feat: 4 (over z).
Axes of the slice: x: 2, y: 2, z: 4, core: 2. Of those that a mesh axis runs over, the one named last changes fastest.
Arguments:
- node_feats: bfloat16 [8192, 512], P('blk', 'feat'), may hold values from -6 to 6
- weight: bfloat16 [512, 512], P(None, 'feat'), may hold values from -0.25 to 0.25
- tile_value: bfloat16 [8, 5, 8, 128, 128], P('blk'), may hold values from -0.75 to 0.75
- tile_row: int32 [8, 5, 8], P('blk'), may hold values from 0 to 7
- tile_col: int32 [8, 5, 8], P('blk'), may hold values from 0 to 7
- tile_count: int32 [8, 5], P('blk'), may hold values from 2 to 8, as said below
- grad_out: bfloat16 [8192, 512], P('blk', 'feat'), may hold values from -6 to 6
Outputs:
- output_y: bfloat16 [8192, 512], P('blk', 'feat')
- grad_x: bfloat16 [8192, 512], P('blk', 'feat')
- grad_w: float32 [512, 512], P(None, 'feat')
The draws below stay inside these ranges and needn't reach their ends.
Inputs may be any that keep to these rules, and one draw needn't show every extreme that they name: `tile_count`: in every draw one owner has all 8 slots live for every distance; owners differ in how many tiles they hold.
All inputs are finite; a program needn't handle non-finite values.
Results may differ from the reference program's by a relative error of at most 0.0062.
Values may be sent and summed in bfloat16 or wider, within the bound.
A program may use at most 64 MiB of HBM per device.

```python
import jax
import jax.numpy as jnp
from jax import lax

D = 512
TB = 128
RB = 8
REACH = 2
SLOTS = 8
OFFS = 5
OWNERS = 8
NODES = 8192


def draw_tile_count(key, part):
    key_base, key_heavy, key_full = jax.random.split(key, 3)
    base_count = jax.random.randint(key_base, (OWNERS, OFFS), SLOTS // 4, SLOTS * 5 // 8 + 1)
    heavy_owner = jax.random.randint(key_heavy, (OWNERS, 1), 0, 4) == 0
    counts_all = jnp.where(heavy_owner, jnp.minimum(base_count * 2, SLOTS), base_count)
    full_owner = jax.random.randint(key_full, (), 0, OWNERS)
    owner_ids = jnp.arange(OWNERS)[:, None]
    counts_all = jnp.where(owner_ids == full_owner, SLOTS, counts_all)
    return counts_all.astype(jnp.int32)


def with_ends(array, own_key, smallest, high):
    place = [jax.random.randint(jax.random.fold_in(own_key, axis), (), 0, length) for axis, length in enumerate(array.shape)]
    longest = array.shape.index(max(array.shape))
    neighbour = place[:longest] + [(place[longest] + 1) % array.shape[longest]] + place[longest + 1:]
    return array.at[tuple(place)].set(smallest).at[tuple(neighbour)].set(high)


def block_scale(stream_key, dims, shards, least, largest):
    def one(axis_at, shards_of):
        heights = jax.random.uniform(jax.random.fold_in(jax.random.fold_in(stream_key, 6), axis_at), (shards_of,), jnp.float32, least / len(shards), largest / len(shards))
        return jnp.repeat(jnp.exp(heights), dims[axis_at] // shards_of).reshape((-1,) + (1,) * (len(dims) - axis_at - 1))

    gain = one(*shards[0])
    for cut in shards[1:]:
        gain = gain * one(*cut)
    return gain


def noise(stream_key, dims, width, reach, pieces=(), kind=jnp.bfloat16):
    gain = block_scale(stream_key, dims, pieces, -0.22, 0.18) if pieces else 1.0
    array = jax.random.normal(stream_key, dims, jnp.float32) * width * gain
    return jnp.minimum(jnp.maximum(array, -reach), reach).astype(kind)


def setup_inputs(seed: int = 0) -> dict:
    arg_keys = jax.random.split(jax.random.key(seed), 8)
    return {
        "node_feats": noise(arg_keys[0], (NODES, D), 1.0, 6.0, ((0, 8), (1, 4))),
        "weight": noise(arg_keys[1], (D, D), D ** -0.5, 0.25, ((1, 4),)),
        "tile_value": noise(arg_keys[2], (OWNERS, OFFS, SLOTS, TB, TB), ((3 * TB) ** -0.5), 0.75, ((0, 8),)),
        "tile_row": with_ends(jax.random.randint(arg_keys[3], (OWNERS, OFFS, SLOTS), 0, RB), jax.random.fold_in(arg_keys[3], 1), 0, RB - 1).astype(jnp.int32),
        "tile_col": with_ends(jax.random.randint(arg_keys[4], (OWNERS, OFFS, SLOTS), 0, RB), jax.random.fold_in(arg_keys[4], 1), 0, RB - 1).astype(jnp.int32),
        "tile_count": draw_tile_count(jax.random.fold_in(arg_keys[7], 71), 0),
        "grad_out": noise(arg_keys[6], (NODES, D), 1.0, 6.0, ((0, 8), (1, 4))),
    }


def reference(node_feats, weight, tile_value, tile_row, tile_col, tile_count, grad_out):
    hidden = jnp.dot(node_feats, weight, preferred_element_type=jnp.float32).astype(jnp.bfloat16)
    hidden_blocks = hidden.reshape(OWNERS, RB, TB, D)
    slot_ids = jnp.arange(SLOTS, dtype=jnp.int32)
    block_ids = jnp.arange(RB, dtype=jnp.int32)

    def forward_one(owner):
        accum_total = jnp.zeros((RB, TB, D), jnp.float32)
        for offset in range(OFFS):
            source = ((owner + offset - REACH) % OWNERS).astype(jnp.int32)
            panel_block = lax.dynamic_index_in_dim(hidden_blocks, source, 0, keepdims=False)
            tile_block = tile_value[owner, offset].astype(jnp.float32)
            picked = jnp.take(panel_block, tile_col[owner, offset], axis=0).astype(jnp.float32)
            product = jnp.einsum('sij,sjf->sif', tile_block, picked, precision=lax.Precision.HIGHEST)
            live_slots = slot_ids < tile_count[owner, offset]
            onehot = ((tile_row[owner, offset][None, :] == block_ids[:, None]) & live_slots[None, :]).astype(jnp.float32)
            accum_total = accum_total + jnp.einsum('rs,sif->rif', onehot, product, precision=lax.Precision.HIGHEST)
        return accum_total

    aggregated = lax.map(forward_one, jnp.arange(OWNERS, dtype=jnp.int32)).reshape(NODES, D)
    preact = aggregated + hidden.astype(jnp.float32)
    output_y = jax.nn.silu(preact).astype(jnp.bfloat16)
    sigmoid_pre = jax.nn.sigmoid(preact)
    slope_term = sigmoid_pre * (1.0 + preact * (1.0 - sigmoid_pre))
    grad_pre = (grad_out.astype(jnp.float32) * slope_term).astype(jnp.bfloat16)
    grad_blocks = grad_pre.reshape(OWNERS, RB, TB, D)

    def backward_one(target):
        accum_total = jnp.zeros((RB, TB, D), jnp.float32)
        for offset in range(OFFS):
            owner = ((target - offset + REACH) % OWNERS).astype(jnp.int32)
            tile_block = lax.dynamic_index_in_dim(tile_value[:, offset], owner, 0, keepdims=False).astype(jnp.float32)
            rows_here = lax.dynamic_index_in_dim(tile_row[:, offset], owner, 0, keepdims=False)
            cols_here = lax.dynamic_index_in_dim(tile_col[:, offset], owner, 0, keepdims=False)
            count_here = lax.dynamic_index_in_dim(tile_count[:, offset], owner, 0, keepdims=False)
            owner_grads = lax.dynamic_index_in_dim(grad_blocks, owner, 0, keepdims=False)
            picked = jnp.take(owner_grads, rows_here, axis=0).astype(jnp.float32)
            product = jnp.einsum('sji,sjf->sif', tile_block, picked, precision=lax.Precision.HIGHEST)
            live_slots = slot_ids < count_here
            onehot = ((cols_here[None, :] == block_ids[:, None]) & live_slots[None, :]).astype(jnp.float32)
            accum_total = accum_total + jnp.einsum('cs,sif->cif', onehot, product, precision=lax.Precision.HIGHEST)
        return accum_total

    transposed = lax.map(backward_one, jnp.arange(OWNERS, dtype=jnp.int32)).reshape(NODES, D)
    grad_hidden = (grad_pre.astype(jnp.float32) + transposed).astype(jnp.bfloat16)
    grad_w = jnp.dot(node_feats.T, grad_hidden, preferred_element_type=jnp.float32)
    grad_x = jnp.dot(grad_hidden, weight.T, preferred_element_type=jnp.float32).astype(jnp.bfloat16)
    return (output_y, grad_x, grad_w)
```

```python
import functools

import jax
import jax.numpy as jnp
from jax import lax
from jax.experimental import pallas as pl
from jax.experimental.pallas import tpu as pltpu
from jax.sharding import PartitionSpec as P

MESH = pl.DeviceIdType.MESH
BF = jnp.bfloat16
F32 = jnp.float32


def stage_factors(count, rows):
    factors = []
    while count > 1:
        size = max(f for f in range(2, 17) if count % f == 0 and rows % (16 * f) == 0)
        factors.append(size)
        count //= size
    return factors


def remote(src, dst, send, recv, where):
    return pltpu.make_async_remote_copy(
        src_ref=src, dst_ref=dst, send_sem=send, recv_sem=recv, device_id=where, device_id_type=MESH
    )


def layer_kernel(
    dims, x, w, tv, tr, tc, cnt, go, y, gx, gw,
    xg, wz, tt, prod, gp, sent, got, gg, gwb, *rest
):
    nb, nz, offs, slots, blocks, side, width, ahead, factors = dims
    stages = len(factors)
    hid, rest = rest[:offs], rest[offs:]
    gathered, summed = rest[:stages], rest[stages : 2 * stages]
    (xs, xr, xl, ws, wr, hs, hr, gs, gr, zs, zr, zl) = rest[2 * stages : 2 * stages + 12]
    psems = rest[2 * stages + 12 :]
    reach = (offs - 1) // 2
    far = [k for k in range(offs) if k != reach]
    per_block = slots // blocks
    me = lax.axis_index("feat")
    own = lax.axis_index("blk")

    def rows(b):
        return pl.ds(pl.multiple_of(b * side, side), side)

    def cols(z):
        return pl.ds(pl.multiple_of(z * width, width), width)

    def blk_at(distance):
        return lax.rem(own + distance + nb, nb)

    def stage_peer(stage, step):
        stride = 1
        for f in factors[:stage]:
            stride *= f
        size = factors[stage]
        digit = lax.rem(own // stride, size)
        other = lax.rem(digit + step, size)
        return digit, other, own + (other - digit) * stride

    barrier = pltpu.get_barrier_semaphore()
    greeted = 0
    for step in range(1, nz):
        pl.semaphore_signal(barrier, inc=1, device_id={"feat": lax.rem(me + step, nz)}, device_id_type=MESH)
        greeted += 1
    for k in far if stages > 1 else ():
        pl.semaphore_signal(barrier, inc=1, device_id={"blk": blk_at(k - reach)}, device_id_type=MESH)
        greeted += 1
    for stage in range(stages):
        for step in range(1, factors[stage]):
            _, _, peer = stage_peer(stage, step)
            pl.semaphore_signal(barrier, inc=1, device_id={"blk": peer}, device_id_type=MESH)
            greeted += 1
    pl.semaphore_wait(barrier, greeted)

    def line_send(src_of, dst, send, recv, b):
        for d in (1, 2):
            for sign in (-1, 1):
                t = me + sign * d

                @pl.when((t >= 0) & (t < nz))
                def _():
                    remote(
                        src_of(b), dst.at[rows(b), cols(me)], send.at[t, b], recv.at[me, b], {"feat": t}
                    ).start()

    def line_recv(dst, relay, recv, b):
        for d in range(1, nz):
            for sign in (-1, 1):
                s = me + sign * d

                @pl.when((s >= 0) & (s < nz))
                def _():
                    piece = dst.at[rows(b), cols(s)]
                    remote(piece, piece, relay.at[s, b], recv.at[s, b], {"feat": s}).wait_recv()
                    if d >= 2:
                        t = me - sign

                        @pl.when((t >= 0) & (t < nz))
                        def _():
                            remote(piece, piece, relay.at[s, b], recv.at[s, b], {"feat": t}).start()

    def line_drain(dst, send, relay, recv, b):
        for d in (1, 2):
            for sign in (-1, 1):
                t = me + sign * d

                @pl.when((t >= 0) & (t < nz))
                def _():
                    piece = dst.at[rows(b), cols(me)]
                    remote(piece, piece, send.at[t, b], recv.at[me, b], {"feat": t}).wait_send()

        for d in range(2, nz):
            for sign in (-1, 1):
                s = me + sign * d
                t = me - sign

                @pl.when((s >= 0) & (s < nz) & (t >= 0) & (t < nz))
                def _():
                    piece = dst.at[rows(b), cols(s)]
                    remote(piece, piece, relay.at[s, b], recv.at[s, b], {"feat": t}).wait_send()

    def x_piece(b):
        return x.at[rows(b), :]

    for b in range(min(ahead, blocks)):
        line_send(x_piece, xg, xs, xr, b)
    for step in range(1, nz):
        d = lax.rem(me + step, nz)
        remote(w.at[cols(d), :], wz.at[:, cols(me)], ws.at[step], wr.at[nz - step], {"feat": d}).start()
    xg[:, cols(me)] = x[...]
    wz[:, cols(me)] = w[cols(me), :]

    def forward_step(b, carry):
        @pl.when(b + ahead < blocks)
        def _():
            line_send(x_piece, xg, xs, xr, b + ahead)

        for k in range(offs):
            for s in range(per_block):
                slot = b * per_block + s
                tt[k, slot] = tv[0, k, slot].T
        line_recv(xg, xl, xr, b)
        hid[reach][b] = jnp.dot(xg[rows(b), :], w[...], preferred_element_type=F32).astype(BF)
        for k in far:
            remote(
                hid[reach].at[b], hid[k].at[b], hs.at[k, b], hr.at[k, b], {"blk": blk_at(reach - k)}
            ).start()
        return carry

    lax.fori_loop(0, blocks, forward_step, 0)

    def forward_products(k):
        for s in range(slots):
            prod[k, s] = jnp.dot(tv[0, k, s], hid[k][tc[0, k, s]], preferred_element_type=F32)

    forward_products(reach)
    for k in far:
        for b in range(blocks):
            remote(
                hid[k].at[b], hid[k].at[b], hs.at[k, b], hr.at[k, b], {"blk": blk_at(k - reach)}
            ).wait_recv()
        forward_products(k)

    def weight_of(table, k, s, b):
        return jnp.where((table[0, k, s] == b) & (s < cnt[0, k]), 1.0, 0.0).astype(F32)

    def pointwise(b, carry):
        v = hid[reach][b].astype(F32)
        for k in range(offs):
            for s in range(slots):
                v = v + prod[k, s] * weight_of(tr, k, s, b)
        sigma = jax.nn.sigmoid(v)
        y[rows(b), :] = (v * sigma).astype(BF)
        slope = sigma * (1.0 + v * (1.0 - sigma))
        gp[b] = (go[rows(b), :].astype(F32) * slope).astype(BF)
        return carry

    lax.fori_loop(0, blocks, pointwise, 0)

    for k in range(offs):
        for s in range(slots):
            prod[k, s] = jnp.dot(tt[k, s], gp[tr[0, k, s]], preferred_element_type=F32)

    def column_sum(k, c, start):
        total = start
        for s in range(slots):
            term = prod[k, s] * weight_of(tc, k, s, c)
            total = term if total is None else total + term
        return total

    gw[...] = jnp.zeros_like(gw)

    def gg_piece(b):
        return gg.at[rows(b), cols(me)]

    def make_grad(b):
        total = column_sum(reach, b, gp[b].astype(F32))
        for k in far:
            remote(
                sent.at[k, b], got.at[k, b], gs.at[k, b], gr.at[k, b], {"blk": blk_at(reach - k)}
            ).wait_recv()
            total = total + got[k, b].astype(F32)
        grad = total.astype(BF)
        gg[rows(b), cols(me)] = grad
        line_send(gg_piece, gg, zs, zr, b)
        gw[...] += lax.dot_general(
            xg[rows(b), :], grad, (((0,), (0,)), ((), ())), preferred_element_type=F32
        )

    def finish(b):
        line_recv(gg, zl, zr, b)
        gx[rows(b), :] = lax.dot_general(
            gg[rows(b), :], wz[...], (((1,), (1,)), ((), ())), preferred_element_type=F32
        ).astype(BF)

    for step in range(1, nz):
        d = lax.rem(me + step, nz)
        piece = wz.at[:, cols(d)]
        remote(w.at[cols(d), :], piece, ws.at[step], wr.at[step], {"feat": d}).wait_recv()

    lag, tail = 1, 3

    def backward_step(c, carry):
        @pl.when(c < blocks)
        def _():
            for k in far:
                sent[k, c] = column_sum(k, c, None).astype(BF)
                remote(
                    sent.at[k, c], got.at[k, c], gs.at[k, c], gr.at[k, c], {"blk": blk_at(k - reach)}
                ).start()

        @pl.when(c >= lag)
        def _():
            make_grad(c - lag)

        @pl.when(c >= tail)
        def _():
            finish(c - tail)

        return carry

    lax.fori_loop(0, blocks + lag, backward_step, 0)

    gwb[...] = gw[...].astype(BF)
    height = gw.shape[0]
    for stage in range(stages):
        size = factors[stage]
        chunk = height // size
        src, buf, out = gwb if stage == 0 else summed[stage - 1], gathered[stage], summed[stage]
        rs_s, rs_r, ag_s, ag_r = psems[4 * stage : 4 * stage + 4]

        def part(q):
            return pl.ds(pl.multiple_of(q * chunk, chunk), chunk)

        for step in range(1, size):
            _, other, peer = stage_peer(stage, step)
            remote(src.at[part(other), :], buf.at[step], rs_s.at[step], rs_r.at[step], {"blk": peer}).start()
        if stage == 0:
            for b in range(blocks + lag - tail, blocks):
                finish(b)
        digit, _, _ = stage_peer(stage, 1)
        if stage == 0:
            total = gw[part(digit), :]
        else:
            total = src[part(digit), :].astype(F32)
        for step in range(1, size):
            _, _, peer = stage_peer(stage, step)
            remote(buf.at[step], buf.at[step], rs_s.at[step], rs_r.at[step], {"blk": peer}).wait_recv()
            total = total + buf[step].astype(F32)
        out[part(digit), :] = total.astype(BF)
        for step in range(1, size):
            _, _, peer = stage_peer(stage, step)
            piece = out.at[part(digit), :]
            remote(piece, piece, ag_s.at[step], ag_r.at[step], {"blk": peer}).start()
        for step in range(1, size):
            _, other, peer = stage_peer(stage, size - step)
            piece = out.at[part(other), :]
            remote(piece, piece, ag_s.at[step], ag_r.at[step], {"blk": peer}).wait_recv()
    gw[...] = (summed[-1] if stages else gwb)[...].astype(F32)

    for stage in range(stages):
        size = factors[stage]
        chunk = height // size
        src, buf, out = gwb if stage == 0 else summed[stage - 1], gathered[stage], summed[stage]
        rs_s, rs_r, ag_s, ag_r = psems[4 * stage : 4 * stage + 4]
        for step in range(1, size):
            _, other, peer = stage_peer(stage, step)
            remote(buf.at[step], buf.at[step], rs_s.at[step], rs_r.at[step], {"blk": peer}).wait_send()
            remote(buf.at[step], buf.at[step], ag_s.at[step], ag_r.at[step], {"blk": peer}).wait_send()
    for step in range(1, nz):
        d = lax.rem(me + step, nz)
        remote(w.at[cols(d), :], wz.at[:, cols(me)], ws.at[step], wr.at[step], {"feat": d}).wait_send()

    def drain(b, carry):
        line_drain(xg, xs, xl, xr, b)
        line_drain(gg, zs, zl, zr, b)
        for k in far:
            remote(hid[k].at[b], hid[k].at[b], hs.at[k, b], hr.at[k, b], {"blk": blk_at(reach - k)}).wait_send()
            remote(sent.at[k, b], got.at[k, b], gs.at[k, b], gr.at[k, b], {"blk": blk_at(k - reach)}).wait_send()
        return carry

    lax.fori_loop(0, blocks, drain, 0)


def on_device(nb, nz, x, w, tv, tr, tc, cnt, go):
    offs, slots, side = tv.shape[1], tv.shape[2], tv.shape[-1]
    height, width = x.shape
    blocks = height // side
    depth, out_width = w.shape
    factors = stage_factors(nb, depth)
    dims = (nb, nz, offs, slots, blocks, side, width, 3, tuple(factors))
    vmem = pl.BlockSpec(memory_space=pltpu.VMEM)
    smem = pl.BlockSpec(memory_space=pltpu.SMEM)
    dma = pltpu.SemaphoreType.DMA
    psems = []
    for f in factors:
        psems += [dma((f,))] * 4
    line = [dma((nz, blocks))] * 3
    banded = [dma((offs, blocks))] * 2
    return pl.pallas_call(
        functools.partial(layer_kernel, dims),
        out_shape=(
            jax.ShapeDtypeStruct((height, out_width), BF),
            jax.ShapeDtypeStruct((height, width), BF),
            jax.ShapeDtypeStruct((depth, out_width), F32),
        ),
        in_specs=[vmem, vmem, vmem, smem, smem, smem, vmem],
        out_specs=(vmem, vmem, vmem),
        scratch_shapes=[
            pltpu.VMEM((height, nz * width), BF),
            pltpu.VMEM((width, nz * out_width), BF),
            pltpu.VMEM((offs, slots, side, side), BF),
            pltpu.VMEM((offs, slots, side, out_width), F32),
            pltpu.VMEM((blocks, side, out_width), BF),
            pltpu.VMEM((offs, blocks, side, out_width), BF),
            pltpu.VMEM((offs, blocks, side, out_width), BF),
            pltpu.VMEM((height, nz * out_width), BF),
            pltpu.VMEM((depth, out_width), BF),
        ]
        + [pltpu.VMEM((blocks, side, out_width), BF)] * offs
        + [pltpu.VMEM((f, depth // f, out_width), BF) for f in factors]
        + [pltpu.VMEM((depth, out_width), BF) for f in factors]
        + line
        + [dma((nz,)), dma((nz,))]
        + banded
        + banded
        + line
        + psems,
        compiler_params=pltpu.CompilerParams(
            collective_id=0, has_side_effects=True, vmem_limit_bytes=40 * 1024 * 1024
        ),
    )(x, w, tv, tr, tc, cnt, go)


def solution(mesh):
    return jax.shard_map(
        functools.partial(on_device, mesh.shape["blk"], mesh.shape["feat"]),
        mesh=mesh,
        in_specs=(
            P("blk", "feat"),
            P(None, "feat"),
            P("blk", None, None, None, None),
            P("blk", None, None),
            P("blk", None, None),
            P("blk", None),
            P("blk", "feat"),
        ),
        out_specs=(P("blk", "feat"), P("blk", "feat"), P(None, "feat")),
        check_vma=False,
    )
```

```python
import functools

import jax
import jax.numpy as jnp
from jax import lax
from jax.experimental import pallas as pl
from jax.experimental.pallas import tpu as pltpu
from jax.sharding import PartitionSpec as P

MESH = pl.DeviceIdType.MESH
BF = jnp.bfloat16
F32 = jnp.float32


def stage_factors(count, rows):
    factors = []
    while count > 1:
        size = max(f for f in range(2, 17) if count % f == 0 and rows % (16 * f) == 0)
        factors.append(size)
        count //= size
    return factors


def remote(src, dst, send, recv, where):
    return pltpu.make_async_remote_copy(
        src_ref=src, dst_ref=dst, send_sem=send, recv_sem=recv, device_id=where, device_id_type=MESH
    )


def layer_kernel(
    dims, x, w_in, tv_in, tr, tc, cnt, go_in, y, gx, gw,
    xg, wz, w, tv, go, tt, prod, gp, sent, got, gg, gwb, *rest
):
    nb, nz, offs, slots, blocks, side, width, ahead, factors = dims
    stages = len(factors)
    hid, rest = rest[:offs], rest[offs:]
    gathered, summed = rest[:stages], rest[stages : 2 * stages]
    (xs, xr, xl, ws, wr, hs, hr, gs, gr, zs, zr, zl, near) = rest[2 * stages : 2 * stages + 13]
    psems = rest[2 * stages + 13 :]
    reach = (offs - 1) // 2
    per_block = slots // blocks
    me = lax.axis_index("feat")
    own = lax.axis_index("blk")
    turn = 1 - 2 * lax.rem(own, 2)
    OWN, PAIR, CROSS, AHEAD, BEHIND = range(5)
    lean = (0, 1, -1, 2, -2)

    def offset_of(role):
        return reach + lean[role] * turn

    def owner_at(role):
        return {"blk": lax.rem(own + lean[role] * turn + nb, nb)}

    local = [
        pltpu.make_async_copy(w_in, w, near.at[0]),
        pltpu.make_async_copy(x, xg.at[:, pl.ds(pl.multiple_of(me * width, width), width)], near.at[1]),
        pltpu.make_async_copy(
            w_in.at[pl.ds(pl.multiple_of(me * width, width), width), :],
            wz.at[:, pl.ds(pl.multiple_of(me * w.shape[1], w.shape[1]), w.shape[1])],
            near.at[2],
        ),
        pltpu.make_async_copy(tv_in.at[0], tv, near.at[3]),
        pltpu.make_async_copy(go_in, go, near.at[4]),
    ]
    for copy in local:
        copy.start()

    def rows(b):
        return pl.ds(pl.multiple_of(b * side, side), side)

    def cols(z):
        return pl.ds(pl.multiple_of(z * width, width), width)

    def stage_peer(stage, step):
        stride = 1
        for f in factors[:stage]:
            stride *= f
        size = factors[stage]
        digit = lax.rem(own // stride, size)
        other = lax.rem(digit + step, size)
        return digit, other, own + (other - digit) * stride

    barrier = pltpu.get_barrier_semaphore()
    greeted = 0
    for step in range(1, nz):
        pl.semaphore_signal(barrier, inc=1, device_id={"feat": lax.rem(me + step, nz)}, device_id_type=MESH)
        greeted += 1
    for role in (PAIR, AHEAD, BEHIND) if stages > 1 else ():
        pl.semaphore_signal(barrier, inc=1, device_id=owner_at(role), device_id_type=MESH)
        greeted += 1
    for stage in range(stages):
        for step in range(1, factors[stage]):
            _, _, peer = stage_peer(stage, step)
            pl.semaphore_signal(barrier, inc=1, device_id={"blk": peer}, device_id_type=MESH)
            greeted += 1
    pl.semaphore_wait(barrier, greeted)

    def line_send(src_of, dst, send, recv, b):
        for d in (1, 2):
            for sign in (-1, 1):
                t = me + sign * d

                @pl.when((t >= 0) & (t < nz))
                def _():
                    remote(
                        src_of(b), dst.at[rows(b), cols(me)], send.at[t, b], recv.at[me, b], {"feat": t}
                    ).start()

    def line_recv(dst, relay, recv, b):
        for d in range(1, nz):
            for sign in (-1, 1):
                s = me + sign * d

                @pl.when((s >= 0) & (s < nz))
                def _():
                    piece = dst.at[rows(b), cols(s)]
                    remote(piece, piece, relay.at[s, b], recv.at[s, b], {"feat": s}).wait_recv()
                    if d >= 2:
                        t = me - sign

                        @pl.when((t >= 0) & (t < nz))
                        def _():
                            remote(piece, piece, relay.at[s, b], recv.at[s, b], {"feat": t}).start()

    def line_drain(dst, send, relay, recv, b):
        for d in (1, 2):
            for sign in (-1, 1):
                t = me + sign * d

                @pl.when((t >= 0) & (t < nz))
                def _():
                    piece = dst.at[rows(b), cols(me)]
                    remote(piece, piece, send.at[t, b], recv.at[me, b], {"feat": t}).wait_send()

        for d in range(2, nz):
            for sign in (-1, 1):
                s = me + sign * d
                t = me - sign

                @pl.when((s >= 0) & (s < nz) & (t >= 0) & (t < nz))
                def _():
                    piece = dst.at[rows(b), cols(s)]
                    remote(piece, piece, relay.at[s, b], recv.at[s, b], {"feat": t}).wait_send()

    def x_piece(b):
        return x.at[rows(b), :]

    for b in range(min(ahead, blocks)):
        line_send(x_piece, xg, xs, xr, b)
    for step in range(1, nz):
        d = lax.rem(me + step, nz)
        remote(w_in.at[cols(d), :], wz.at[:, cols(me)], ws.at[step], wr.at[nz - step], {"feat": d}).start()
    for copy in local[:4]:
        copy.wait()

    landing = {PAIR: PAIR, AHEAD: BEHIND, BEHIND: AHEAD}

    def hid_copy(role, b):
        return remote(hid[OWN].at[b], hid[landing[role]].at[b], hs.at[role, b], hr.at[landing[role], b], owner_at(role))

    def hid_wait(role, b):
        remote(hid[role].at[b], hid[role].at[b], hs.at[role, b], hr.at[role, b], owner_at(PAIR)).wait_recv()

    def hid_passed(b):
        return remote(hid[AHEAD].at[b], hid[CROSS].at[b], hs.at[CROSS, b], hr.at[CROSS, b], owner_at(PAIR))

    def hid_relay(b):
        hid_wait(AHEAD, b)
        hid_passed(b).start()

    def forward_step(b, carry):
        @pl.when(b + ahead < blocks)
        def _():
            line_send(x_piece, xg, xs, xr, b + ahead)

        for role in range(offs):
            for s in range(per_block):
                slot = b * per_block + s
                tt[role, slot] = tv[offset_of(role), slot].T
        line_recv(xg, xl, xr, b)
        hid[OWN][b] = jnp.dot(xg[rows(b), :], w[...], preferred_element_type=F32).astype(BF)
        hid_copy(PAIR, b).start()
        hid_copy(AHEAD, b).start()
        hid_copy(BEHIND, b).start()

        @pl.when(b >= 1)
        def _():
            hid_relay(b - 1)

        return carry

    lax.fori_loop(0, blocks, forward_step, 0)

    hid_relay(blocks - 1)

    def forward_products(role):
        k = offset_of(role)
        for s in range(slots):
            prod[role, s] = jnp.dot(tv[k, s], hid[role][tc[k, 0, s]], preferred_element_type=F32)

    forward_products(OWN)
    forward_products(AHEAD)
    for role in (PAIR, BEHIND, CROSS):
        for b in range(blocks):
            hid_wait(role, b)
        forward_products(role)
    local[4].wait()

    def weight_of(table, k, s, b):
        return jnp.where((table[k, 0, s] == b) & (s < cnt[0, k]), 1.0, 0.0).astype(F32)

    def pointwise(b, carry):
        v = hid[OWN][b].astype(F32)
        for role in range(offs):
            for s in range(slots):
                v = v + prod[role, s] * weight_of(tr, offset_of(role), s, b)
        sigma = jax.nn.sigmoid(v)
        y[rows(b), :] = (v * sigma).astype(BF)
        slope = sigma * (1.0 + v * (1.0 - sigma))
        gp[b] = (go[rows(b), :].astype(F32) * slope).astype(BF)
        return carry

    lax.fori_loop(0, blocks, pointwise, 0)

    for role in range(offs):
        for s in range(slots):
            prod[role, s] = jnp.dot(tt[role, s], gp[tr[offset_of(role), 0, s]], preferred_element_type=F32)

    def column_sum(role, c, start):
        total = start
        for s in range(slots):
            term = prod[role, s] * weight_of(tc, offset_of(role), s, c)
            total = term if total is None else total + term
        return total

    target = {PAIR: PAIR, CROSS: PAIR, AHEAD: AHEAD, BEHIND: BEHIND}
    arrives = {PAIR: PAIR, CROSS: CROSS, AHEAD: BEHIND, BEHIND: AHEAD}

    def sum_copy(role, c):
        return remote(
            sent.at[role, c], got.at[arrives[role], c], gs.at[role, c], gr.at[arrives[role], c], owner_at(target[role])
        )

    def sum_wait(role, c):
        remote(got.at[role, c], got.at[role, c], gs.at[role, c], gr.at[role, c], owner_at(PAIR)).wait_recv()

    def send_sum(role, c):
        sent[role, c] = column_sum(role, c, None).astype(BF)
        sum_copy(role, c).start()

    def send_joint(c):
        sum_wait(CROSS, c)
        sent[AHEAD, c] = column_sum(AHEAD, c, got[CROSS, c].astype(F32)).astype(BF)
        sum_copy(AHEAD, c).start()

    gw[...] = jnp.zeros_like(gw)

    def gg_piece(b):
        return gg.at[rows(b), cols(me)]

    def make_grad(b):
        total = column_sum(OWN, b, gp[b].astype(F32))
        for role in (PAIR, BEHIND, AHEAD):
            sum_wait(role, b)
            total = total + got[role, b].astype(F32)
        grad = total.astype(BF)
        gg[rows(b), cols(me)] = grad
        line_send(gg_piece, gg, zs, zr, b)
        gw[...] += lax.dot_general(
            xg[rows(b), :], grad, (((0,), (0,)), ((), ())), preferred_element_type=F32
        )

    def finish(b):
        line_recv(gg, zl, zr, b)
        gx[rows(b), :] = lax.dot_general(
            gg[rows(b), :], wz[...], (((1,), (1,)), ((), ())), preferred_element_type=F32
        ).astype(BF)

    for step in range(1, nz):
        d = lax.rem(me + step, nz)
        piece = wz.at[:, cols(d)]
        remote(w_in.at[cols(d), :], piece, ws.at[step], wr.at[step], {"feat": d}).wait_recv()

    lag, tail = 2, 4

    def backward_step(c, carry):
        @pl.when(c < blocks)
        def _():
            send_sum(CROSS, c)
            send_sum(BEHIND, c)
            send_sum(PAIR, c)

        @pl.when((c >= 1) & (c <= blocks))
        def _():
            send_joint(c - 1)

        @pl.when(c >= lag)
        def _():
            make_grad(c - lag)

        @pl.when(c >= tail)
        def _():
            finish(c - tail)

        return carry

    lax.fori_loop(0, blocks + lag, backward_step, 0)

    gwb[...] = gw[...].astype(BF)
    height = gw.shape[0]
    for stage in range(stages):
        size = factors[stage]
        chunk = height // size
        src, buf, out = gwb if stage == 0 else summed[stage - 1], gathered[stage], summed[stage]
        rs_s, rs_r, ag_s, ag_r = psems[4 * stage : 4 * stage + 4]

        def part(q):
            return pl.ds(pl.multiple_of(q * chunk, chunk), chunk)

        for step in range(1, size):
            _, other, peer = stage_peer(stage, step)
            remote(src.at[part(other), :], buf.at[step], rs_s.at[step], rs_r.at[step], {"blk": peer}).start()
        if stage == 0:
            for b in range(blocks + lag - tail, blocks):
                finish(b)
        digit, _, _ = stage_peer(stage, 1)
        if stage == 0:
            total = gw[part(digit), :]
        else:
            total = src[part(digit), :].astype(F32)
        for step in range(1, size):
            _, _, peer = stage_peer(stage, step)
            remote(buf.at[step], buf.at[step], rs_s.at[step], rs_r.at[step], {"blk": peer}).wait_recv()
            total = total + buf[step].astype(F32)
        out[part(digit), :] = total.astype(BF)
        for step in range(1, size):
            _, _, peer = stage_peer(stage, step)
            piece = out.at[part(digit), :]
            remote(piece, piece, ag_s.at[step], ag_r.at[step], {"blk": peer}).start()
        for step in range(1, size):
            _, other, peer = stage_peer(stage, size - step)
            piece = out.at[part(other), :]
            remote(piece, piece, ag_s.at[step], ag_r.at[step], {"blk": peer}).wait_recv()
    gw[...] = (summed[-1] if stages else gwb)[...].astype(F32)

    for stage in range(stages):
        size = factors[stage]
        chunk = height // size
        src, buf, out = gwb if stage == 0 else summed[stage - 1], gathered[stage], summed[stage]
        rs_s, rs_r, ag_s, ag_r = psems[4 * stage : 4 * stage + 4]
        for step in range(1, size):
            _, other, peer = stage_peer(stage, step)
            remote(buf.at[step], buf.at[step], rs_s.at[step], rs_r.at[step], {"blk": peer}).wait_send()
            remote(buf.at[step], buf.at[step], ag_s.at[step], ag_r.at[step], {"blk": peer}).wait_send()
    for step in range(1, nz):
        d = lax.rem(me + step, nz)
        remote(w_in.at[cols(d), :], wz.at[:, cols(me)], ws.at[step], wr.at[step], {"feat": d}).wait_send()

    def drain(b, carry):
        line_drain(xg, xs, xl, xr, b)
        line_drain(gg, zs, zl, zr, b)
        for role in (PAIR, AHEAD, BEHIND):
            hid_copy(role, b).wait_send()
        hid_passed(b).wait_send()
        for role in (PAIR, CROSS, AHEAD, BEHIND):
            sum_copy(role, b).wait_send()
        return carry

    lax.fori_loop(0, blocks, drain, 0)


def on_device(nb, nz, x, w, tv, tr, tc, cnt, go):
    offs, slots, side = tv.shape[1], tv.shape[2], tv.shape[-1]
    height, width = x.shape
    blocks = height // side
    depth, out_width = w.shape
    factors = stage_factors(nb, depth)
    dims = (nb, nz, offs, slots, blocks, side, width, 3, tuple(factors))
    vmem = pl.BlockSpec(memory_space=pltpu.VMEM)
    hbm = pl.BlockSpec(memory_space=pltpu.HBM)
    smem = pl.BlockSpec(memory_space=pltpu.SMEM)
    dma = pltpu.SemaphoreType.DMA
    psems = []
    for f in factors:
        psems += [dma((f,))] * 4
    line = [dma((nz, blocks))] * 3
    banded = [dma((offs, blocks))] * 2
    return pl.pallas_call(
        functools.partial(layer_kernel, dims),
        out_shape=(
            jax.ShapeDtypeStruct((height, out_width), BF),
            jax.ShapeDtypeStruct((height, width), BF),
            jax.ShapeDtypeStruct((depth, out_width), F32),
        ),
        in_specs=[hbm, hbm, hbm, smem, smem, smem, hbm],
        out_specs=(vmem, vmem, vmem),
        scratch_shapes=[
            pltpu.VMEM((height, nz * width), BF),
            pltpu.VMEM((width, nz * out_width), BF),
            pltpu.VMEM((depth, out_width), BF),
            pltpu.VMEM((offs, slots, side, side), BF),
            pltpu.VMEM((height, out_width), BF),
            pltpu.VMEM((offs, slots, side, side), BF),
            pltpu.VMEM((offs, slots, side, out_width), F32),
            pltpu.VMEM((blocks, side, out_width), BF),
            pltpu.VMEM((offs, blocks, side, out_width), BF),
            pltpu.VMEM((offs, blocks, side, out_width), BF),
            pltpu.VMEM((height, nz * out_width), BF),
            pltpu.VMEM((depth, out_width), BF),
        ]
        + [pltpu.VMEM((blocks, side, out_width), BF)] * offs
        + [pltpu.VMEM((f, depth // f, out_width), BF) for f in factors]
        + [pltpu.VMEM((depth, out_width), BF) for f in factors]
        + line
        + [dma((nz,)), dma((nz,))]
        + banded
        + banded
        + line
        + [dma((5,))]
        + psems,
        compiler_params=pltpu.CompilerParams(
            collective_id=0, has_side_effects=True, vmem_limit_bytes=63 * 1024 * 1024
        ),
    )(x, w, tv, jnp.swapaxes(tr, 0, 1), jnp.swapaxes(tc, 0, 1), cnt, go)


def solution(mesh):
    return jax.shard_map(
        functools.partial(on_device, mesh.shape["blk"], mesh.shape["feat"]),
        mesh=mesh,
        in_specs=(
            P("blk", "feat"),
            P(None, "feat"),
            P("blk", None, None, None, None),
            P("blk", None, None),
            P("blk", None, None),
            P("blk", None),
            P("blk", "feat"),
        ),
        out_specs=(P("blk", "feat"), P("blk", "feat"), P(None, "feat")),
        check_vma=False,
    )
```
